32 devices in a mesh: groups: 2 (over y), expert: 16 (over z, x, core).
Axes of the slice: x: 2, y: 2, z: 4, core: 2. Of those that a mesh axis runs over, the one named last changes fastest.
Arguments:
- hidden_act: bfloat16 [28672, 768], P(('groups', 'expert')), parts along dimension 0, may hold values from -0.29882812 to 0.29882812
- out_grad: bfloat16 [28672, 2048], P(('groups', 'expert')), parts along dimension 0, may hold values from -3.59375 to 3.59375
- w_down: bfloat16 [16, 768, 2048], P('expert'), may hold values from -0.125 to 0.125
- block_expert: int32 [32, 7], P(('groups', 'expert')), parts along dimension 0, may hold values from 0 to 15, as said below
- block_count: int32 [32], P(('groups', 'expert')), parts along dimension 0, may hold values from 2 to 7, as said below
Outputs:
- grad_hidden: bfloat16 [28672, 768], P(('groups', 'expert')), parts along dimension 0
- grad_weight: bfloat16 [32, 768, 2048], P(('groups', 'expert')), parts along dimension 0
The draws below stay inside these ranges and needn't reach their ends.
There are 2 independent parts, one for each index of `groups`. The reference program is written for one: setup_inputs(seed, part) draws one part's arguments, and reference() takes and returns one part's arrays. A program takes and returns all parts, laid end to end along the dimension named above; an argument that names none is the same for every part. Nothing has to cross between parts.
Inputs may be any that keep to these rules, and one draw needn't show every extreme that they name: block_expert[e, i] is e or e's partner (e + 8) mod 16, and is e in slots that are not live. Of each pair of partners one is hot: all 7 slots live and all own; the other has at least one own and at least one lent live slot, and at most 4 lent ones. Some device has exactly 4 lent slots. `block_count`: hot devices have 7 live slots.
All inputs are finite; a program needn't handle non-finite values.
Results may differ from the reference program's by a relative error of at most 0.001.
Values may be sent and summed in bfloat16 or wider, within the bound.
No kernel may reach another device: no remote copies, remote signals or barrier semaphores. Data moves between devices by JAX's collectives and lax.ppermute only.
A program may use at most 64 MiB of HBM per device.

```python
import jax
import jax.numpy as jnp
from jax import lax

D = 2048
FF = 768
EXPERTS = 16
BLOCK_ROWS = 128
BLOCKS = 7
LENT_MAX = 4
ROWS = 14336


def pairing_table(key):
    half_way = EXPERTS // 2
    base_key = jax.random.fold_in(key, 7)
    key_hot, key_own, key_lent, key_score = jax.random.split(base_key, 4)
    hot_upper = jax.random.randint(key_hot, (half_way,), 0, 2)
    device = jnp.arange(EXPERTS, dtype=jnp.int32)
    pair_index = device % half_way
    upper_half = (device >= half_way).astype(jnp.int32)
    is_hot = upper_half == hot_upper[pair_index]
    own_count = jax.random.randint(key_own, (EXPERTS,), 1, BLOCKS - LENT_MAX + 1)
    lent_count = jax.random.randint(key_lent, (EXPERTS,), (LENT_MAX + 1) // 2, LENT_MAX + 1)
    lent_count = jnp.where(pair_index == 0, LENT_MAX, lent_count)
    live_count = jnp.where(is_hot, BLOCKS, own_count + lent_count)
    lent_count = jnp.where(is_hot, 0, lent_count)
    slot_ids = jnp.arange(BLOCKS, dtype=jnp.int32)
    scores = jax.random.randint(key_score, (EXPERTS, BLOCKS), 0, 2 ** 20) * BLOCKS + slot_ids[None, :]
    live_mask = slot_ids[None, :] < live_count[:, None]
    rank_live = jnp.sum((live_mask[:, None, :] & (scores[:, None, :] < scores[:, :, None])).astype(jnp.int32), axis=2)
    borrowed = live_mask & (rank_live < lent_count[:, None])
    partner = (device + half_way) % EXPERTS
    expert_table = jnp.where(borrowed, partner[:, None], device[:, None])
    return (expert_table.astype(jnp.int32), live_count.astype(jnp.int32))


def draw_block_expert(key, part):
    return pairing_table(key)[0]


def draw_block_count(key, part):
    return pairing_table(key)[1]


def steps_of(key, shape, shards, low, high):
    level = 1.0
    for dim, parts in shards:
        draws = jax.random.uniform(jax.random.fold_in(jax.random.fold_in(key, 6), dim), (parts,), jnp.float32, low / len(shards), high / len(shards))
        level = level * jnp.repeat(jnp.exp(draws), shape[dim] // parts).reshape((-1,) + (1,) * (len(shape) - 1 - dim))
    return level


def gaussian(stream_key, extent, spread, reach, cuts=(), kind=jnp.bfloat16):
    factor_of = steps_of(stream_key, extent, cuts, -0.22, 0.18) if cuts else 1.0
    values = jax.random.normal(stream_key, extent, jnp.float32) * spread * factor_of
    return jnp.minimum(jnp.maximum(values, -reach), reach).astype(kind)


def setup_inputs(seed: int = 0, part: int = 0) -> dict:
    key_of = jax.random.split(jax.random.key(seed), 6)
    part_keys = jax.random.split(jax.random.fold_in(key_of[5], part), 6)
    hidden_act = gaussian(part_keys[0], (ROWS, FF), 0.05, 0.29882812, ((0, 16),))
    out_grad = gaussian(part_keys[1], (ROWS, D), 0.6, 3.59375, ((0, 16),))
    w_down = gaussian(key_of[2], (EXPERTS, FF, D), D ** -0.5, 0.125, ((0, 16),))
    block_expert = draw_block_expert(jax.random.fold_in(jax.random.fold_in(key_of[5], part), 71), part)
    block_count = draw_block_count(jax.random.fold_in(jax.random.fold_in(key_of[5], part), 71), part)
    return dict(hidden_act=hidden_act, out_grad=out_grad, w_down=w_down, block_expert=block_expert, block_count=block_count)


def reference(hidden_act, out_grad, w_down, block_expert, block_count):
    half_way = EXPERTS // 2
    hid_all = hidden_act.reshape(EXPERTS, BLOCKS, BLOCK_ROWS, FF)
    grad_all = out_grad.reshape(EXPERTS, BLOCKS, BLOCK_ROWS, D)

    def per_device(device):
        hid_dev = hid_all[device]
        grad_dev = grad_all[device]
        slot_ids = jnp.arange(BLOCKS, dtype=jnp.int32)
        live_mask = slot_ids < block_count[device]
        own_mask = live_mask & (block_expert[device] == device)
        lent_mask = live_mask & (block_expert[device] != device)
        own_weight = w_down[device]
        partner_weight = w_down[(device + half_way) % EXPERTS]
        grad_flat = grad_dev.reshape(BLOCKS * BLOCK_ROWS, D)
        dh_own = jnp.dot(grad_flat, own_weight.T, preferred_element_type=jnp.float32).reshape(BLOCKS, BLOCK_ROWS, FF)
        dh_lent = jnp.dot(grad_flat, partner_weight.T, preferred_element_type=jnp.float32).reshape(BLOCKS, BLOCK_ROWS, FF)
        dh_rows = jnp.where(own_mask[:, None, None], dh_own, jnp.where(lent_mask[:, None, None], dh_lent, jnp.float32(0.0)))
        dh_rows = dh_rows.astype(jnp.bfloat16).reshape(BLOCKS * BLOCK_ROWS, FF)
        zero_value = jnp.zeros((), jnp.bfloat16)
        hid_own = jnp.where(own_mask[:, None, None], hid_dev, zero_value).reshape(BLOCKS * BLOCK_ROWS, FF)
        hid_lent = jnp.where(lent_mask[:, None, None], hid_dev, zero_value).reshape(BLOCKS * BLOCK_ROWS, FF)
        dw_own = jnp.dot(hid_own.T, grad_flat, preferred_element_type=jnp.float32)
        dw_lent = jnp.dot(hid_lent.T, grad_flat, preferred_element_type=jnp.float32)
        return dh_rows, dw_own, dw_lent

    dh_rows, dw_own, dw_lent = lax.map(per_device, jnp.arange(EXPERTS, dtype=jnp.int32))
    grad_hidden = dh_rows.reshape(EXPERTS * BLOCKS * BLOCK_ROWS, FF)
    grad_weight = (dw_own + jnp.roll(dw_lent, half_way, axis=0)).astype(jnp.bfloat16)
    return grad_hidden, grad_weight
```

```python
import jax
import jax.numpy as jnp
from jax import lax
from jax.sharding import PartitionSpec as P


BY_MODEL = (((1,), (1,)), ((), ()))
BY_ROWS = (((0,), (0,)), ((), ()))


def dot(a, b, dims):
    return lax.dot_general(a, b, dims, preferred_element_type=jnp.float32)


def shards(hidden_act, out_grad, w_down, block_expert, block_count):
    half_way = lax.axis_size("expert") // 2
    my_index = lax.axis_index("expert")
    block_total = block_expert.shape[1]
    row_count, width_hidden = hidden_act.shape
    width_model = out_grad.shape[1]
    block_rows = row_count // block_total
    lent_slots = (block_total + 1) // 2
    slot_ids = jnp.arange(block_total, dtype=jnp.int32)
    live_mask = slot_ids < block_count[0]
    own_mask = live_mask & (block_expert[0] == my_index)
    lent_mask = live_mask & (block_expert[0] != my_index)
    lent_order = jnp.cumsum(lent_mask.astype(jnp.int32)) - 1
    target_ids = jnp.arange(lent_slots, dtype=jnp.int32)
    pick_int = (lent_mask[None, :] & (lent_order[None, :] == target_ids[:, None])).astype(jnp.int32)
    source_index = jnp.sum(pick_int * slot_ids[None, :], axis=1)
    lent_count = jnp.sum(lent_mask.astype(jnp.int32))
    lends = lent_count > 0
    upward = lends == (my_index < half_way)
    own_rows = jnp.repeat(own_mask, block_rows)[:, None]
    own_weight = w_down[0]

    def sent_block(x, order):
        return lax.dynamic_slice_in_dim(x, source_index[order] * block_rows, block_rows, 0)

    def placed(grad_hidden, back, order):
        start = source_index[order] * block_rows
        kept = lax.dynamic_slice_in_dim(grad_hidden, start, block_rows, 0)
        return lax.dynamic_update_slice_in_dim(
            grad_hidden, jnp.where(lends, back, kept), start, 0
        )

    def towards(up):
        out = [(i, i + half_way) if up else (i + half_way, i) for i in range(half_way)]
        home = [(b, a) for a, b in out]

        def send(x):
            return lax.ppermute(x, "expert", out)

        def give_back(x):
            return lax.ppermute(x, "expert", home)

        def rest(count):
            def run(peer_grad, peer_hid, own_dh, own_dw):
                grads = [peer_grad] + [send(sent_block(out_grad, i)) for i in range(1, count)]
                hids = [peer_hid] + [send(sent_block(hidden_act, i)) for i in range(1, count)]
                grad_hidden = own_dh
                for i in range(count):
                    peer_dh = dot(grads[i], own_weight, BY_MODEL).astype(jnp.bfloat16)
                    grad_hidden = placed(grad_hidden, give_back(peer_dh), i)
                total = own_dw
                if count > 1:
                    total = total + dot(
                        jnp.concatenate(hids[:-1]), jnp.concatenate(grads[:-1]), BY_ROWS
                    )
                total = total + dot(hids[-1], grads[-1], BY_ROWS)
                return grad_hidden, total.astype(jnp.bfloat16)

            return run

        def run():
            header = send(jnp.full((8, 128), lent_count, jnp.int32))
            peer_grad = send(sent_block(out_grad, 0))
            peer_hid = send(sent_block(hidden_act, 0))
            own_dh = jnp.where(own_rows, dot(out_grad, own_weight, BY_MODEL), 0.0)
            own_dw = dot(jnp.where(own_rows, hidden_act, 0), out_grad, BY_ROWS)
            count = jnp.where(lends, lent_count, header[0, 0])
            return lax.switch(
                count - 1,
                [rest(c) for c in range(1, lent_slots + 1)],
                peer_grad,
                peer_hid,
                own_dh.astype(jnp.bfloat16),
                own_dw,
            )

        return run

    grad_hidden, total_dw = lax.cond(upward, towards(True), towards(False))
    return grad_hidden, total_dw[None]


def solution(mesh):
    in_specs = (
        P(("groups", "expert"), None),
        P(("groups", "expert"), None),
        P("expert", None, None),
        P(("groups", "expert"), None),
        P(("groups", "expert")),
    )
    out_specs = (P(("groups", "expert"), None), P(("groups", "expert"), None, None))
    return jax.shard_map(shards, mesh=mesh, in_specs=in_specs, out_specs=out_specs, check_vma=False)
```

```python
import functools

import jax
import jax.numpy as jnp
from jax import lax
from jax.experimental import pallas as pl
from jax.experimental.pallas import tpu as pltpu
from jax.sharding import PartitionSpec as P


BY_MODEL = (((1,), (1,)), ((), ()))
BY_ROWS = (((0,), (0,)), ((), ()))


def dot(a, b, dims):
    return lax.dot_general(a, b, dims, preferred_element_type=jnp.float32)


def tile_of(width, most):
    return max(t for t in range(128, most + 1, 128) if width % t == 0)


def lent_slot(order, expert_ref, count_ref, index_ref):
    found, seen = jnp.int32(0), jnp.int32(0)
    for slot in range(expert_ref.shape[1]):
        lent = (slot < count_ref[0]) & (expert_ref[0, slot] != index_ref[0])
        found = jnp.where(lent & (seen == order), slot, found)
        seen = seen + lent.astype(jnp.int32)
    return found, seen


def pick_blocks(wanted, table, hidden_act, out_grad, block_rows):
    lent_slots = (table[0].shape[1] + 1) // 2

    def numbers(table_refs):
        return [lent_slot(order, *table_refs) for order in range(lent_slots)]

    def block(x, order):
        def at(i, *table_refs):
            if order >= 0:
                return lent_slot(order, *table_refs)[0], 0
            last = lent_slot(0, *table_refs)[1] - 1
            return lent_slot(last, *table_refs)[0], 0

        return pl.BlockSpec((block_rows, x.shape[1]), at)

    pieces = [(x, order) for group in wanted for x in (out_grad, hidden_act) for order in group]
    shapes = [
        jax.ShapeDtypeStruct((len(group) * block_rows, x.shape[1]), x.dtype)
        for group in wanted
        for x in (out_grad, hidden_act)
    ]
    targets = [
        (k, row)
        for k, group in enumerate([g for g in wanted for _ in range(2)])
        for row in range(len(group))
    ]

    def kernel(expert_ref, count_ref, index_ref, *refs):
        table_refs = (expert_ref, count_ref, index_ref)
        sources, results = refs[: len(pieces)], refs[len(pieces) :]
        for source, (k, row) in zip(sources, targets):
            results[k][row * block_rows : (row + 1) * block_rows] = source[...]
        info_ref, header_ref = results[len(shapes) :]
        for order, (slot, total) in enumerate(numbers(table_refs)):
            info_ref[order + 1] = slot
        info_ref[0] = total
        header_ref[...] = jnp.full(header_ref.shape, total, jnp.int32)

    return pl.pallas_call(
        kernel,
        grid_spec=pltpu.PrefetchScalarGridSpec(
            num_scalar_prefetch=3,
            grid=(1,),
            in_specs=[block(x, order) for x, order in pieces],
            out_specs=[pl.BlockSpec(s.shape, lambda i, *_: (0, 0)) for s in shapes]
            + [
                pl.BlockSpec(memory_space=pltpu.SMEM),
                pl.BlockSpec((8, 128), lambda i, *_: (0, 0)),
            ],
        ),
        out_shape=shapes
        + [
            jax.ShapeDtypeStruct((lent_slots + 1,), jnp.int32),
            jax.ShapeDtypeStruct((8, 128), jnp.int32),
        ],
        name="pick_blocks",
    )(*table, *[x for x, _ in pieces])


def hidden_grad(grad, weight):
    rows, width_model = grad.shape
    width_hidden = weight.shape[0]
    tile = tile_of(width_hidden, 384)

    def kernel(grad_ref, weight_ref, out_ref):
        out_ref[...] = dot(grad_ref[...], weight_ref[...], BY_MODEL).astype(out_ref.dtype)

    return pl.pallas_call(
        kernel,
        grid=(width_hidden // tile,),
        in_specs=[
            pl.BlockSpec((rows, width_model), lambda i: (0, 0)),
            pl.BlockSpec((tile, width_model), lambda i: (i, 0)),
        ],
        out_specs=pl.BlockSpec((rows, tile), lambda i: (0, i)),
        out_shape=jax.ShapeDtypeStruct((rows, width_hidden), grad.dtype),
        cost_estimate=pl.CostEstimate(
            flops=2 * rows * width_model * width_hidden,
            bytes_accessed=2 * (rows + width_hidden) * width_model,
            transcendentals=0,
        ),
        name="hidden_grad",
    )(grad, weight)


def weight_grad(own, hids, grads):
    width_hidden, width_model = own.shape
    tile = tile_of(width_model, 1024)
    amount, rows = len(hids), sum(h.shape[0] for h in hids)

    def kernel(own_ref, *refs):
        hid = jnp.concatenate([r[...] for r in refs[:amount]])
        grad = jnp.concatenate([r[...] for r in refs[amount : 2 * amount]])
        refs[-1][...] = (own_ref[...] + dot(hid, grad, BY_ROWS)).astype(refs[-1].dtype)

    return pl.pallas_call(
        kernel,
        grid=(width_model // tile,),
        in_specs=[pl.BlockSpec((width_hidden, tile), lambda i: (0, i))]
        + [pl.BlockSpec(h.shape, lambda i: (0, 0)) for h in hids]
        + [pl.BlockSpec((g.shape[0], tile), lambda i: (0, i)) for g in grads],
        out_specs=pl.BlockSpec((width_hidden, tile), lambda i: (0, i)),
        out_shape=jax.ShapeDtypeStruct(own.shape, hids[0].dtype),
        cost_estimate=pl.CostEstimate(
            flops=2 * rows * width_model * width_hidden,
            bytes_accessed=6 * width_hidden * width_model,
            transcendentals=0,
        ),
        name="weight_grad",
    )(own, *hids, *grads)


def shards(hidden_act, out_grad, w_down, block_expert, block_count):
    half_way = lax.axis_size("expert") // 2
    my_index = lax.axis_index("expert").astype(jnp.int32)
    block_total = block_expert.shape[1]
    block_rows = hidden_act.shape[0] // block_total
    lent_slots = (block_total + 1) // 2
    own_mask = (jnp.arange(block_total, dtype=jnp.int32) < block_count[0]) & (
        block_expert[0] == my_index
    )
    own_rows = jnp.repeat(own_mask, block_rows)[:, None]
    own_weight = w_down[0]
    table = (block_expert, block_count, my_index[None])
    first_grad, first_hid, info, header = pick_blocks(
        [[0]], table, hidden_act, out_grad, block_rows
    )
    lends = info[0] > 0
    upward = lends == (my_index < half_way)

    def placed(grad_hidden, back, order):
        start = info[order + 1] * block_rows
        kept = lax.dynamic_slice_in_dim(grad_hidden, start, block_rows, 0)
        return lax.dynamic_update_slice_in_dim(
            grad_hidden, jnp.where(lends, back, kept), start, 0
        )

    def towards(up):
        out = [(i, i + half_way) if up else (i + half_way, i) for i in range(half_way)]
        home = [(b, a) for a, b in out]

        def send(x):
            return lax.ppermute(x, "expert", out)

        def give_back(x):
            return lax.ppermute(x, "expert", home)

        def rest(count):
            groups = [[0]] + ([list(range(1, count - 1))] if count > 2 else [])
            groups += [[count - 1]] if count > 1 else []

            def run(between, last, peer_grad, peer_hid, own_dh, own_dw):
                sent = ([between[count]] if count > 2 else []) + ([last] if count > 1 else [])
                grads, hids = [peer_grad], [peer_hid]
                for grad, hid in sent:
                    hids.append(send(hid))
                    grads.append(send(grad))
                grad_hidden = own_dh
                for grad, group in zip(grads, groups):
                    back = give_back(hidden_grad(grad, own_weight))
                    for row, order in enumerate(group):
                        part = back[row * block_rows : (row + 1) * block_rows]
                        grad_hidden = placed(grad_hidden, part, order)
                return grad_hidden, weight_grad(own_dw, hids, grads)

            return run

        def run():
            told = send(header)
            peer_grad = send(first_grad)
            peer_hid = send(first_hid)
            counts = range(3, lent_slots + 1)
            more = pick_blocks(
                [[-1]] + [list(range(1, c - 1)) for c in counts],
                table, hidden_act, out_grad, block_rows,
            )
            last = (more[0], more[1])
            between = {c: (more[2 * k + 2], more[2 * k + 3]) for k, c in enumerate(counts)}
            own_dh = jnp.where(own_rows, dot(out_grad, own_weight, BY_MODEL), 0.0)
            count = jnp.where(lends, info[0], told[0, 0])
            count, own_hid = lax.optimization_barrier(
                (count, jnp.where(own_rows, hidden_act, 0))
            )
            own_dw = dot(own_hid, out_grad, BY_ROWS)
            return lax.switch(
                count - 1,
                [rest(c) for c in range(1, lent_slots + 1)],
                between,
                last,
                peer_grad,
                peer_hid,
                own_dh.astype(jnp.bfloat16),
                own_dw,
            )

        return run

    grad_hidden, total_dw = lax.cond(upward, towards(True), towards(False))
    return grad_hidden, total_dw[None]


def solution(mesh):
    in_specs = (
        P(("groups", "expert"), None),
        P(("groups", "expert"), None),
        P("expert", None, None),
        P(("groups", "expert"), None),
        P(("groups", "expert")),
    )
    out_specs = (P(("groups", "expert"), None), P(("groups", "expert"), None, None))
    return jax.shard_map(shards, mesh=mesh, in_specs=in_specs, out_specs=out_specs, check_vma=False)
```
